512 devices in a mesh: blk: 16 (over x, z_lo, core), dp: 32 (over z_hi, y).
Axes of the slice: x: 4, y: 8, z: 8 (z_hi: 4, z_lo: 2; z = z_hi * 2 + z_lo), core: 2. Of those that a mesh axis runs over, the one named last changes fastest.
Arguments:
- spikes: bfloat16 [4, 16384, 128], P(None, 'blk'), may hold values from 0 to 1, as said below
- rec_weights: bfloat16 [16384, 16384], P('blk', 'dp'), may hold values from -0.046875 to 0.046875
- in_current: float32 [4, 16384, 128], P(None, ('blk', 'dp')), may hold values from -6 to 6
- volt_init: float32 [16384, 128], P(('blk', 'dp')), may hold values from -6 to 6
- adapt_init: float32 [16384, 128], P(('blk', 'dp')), may hold values from 0 to 3
- mem_decay: float32 [16384], P(('blk', 'dp')), may hold values from 0.5 to 0.97
- adapt_decay: float32 [16384], P(('blk', 'dp')), may hold values from 0.7 to 0.99
- adapt_gain: float32 [16384], P(('blk', 'dp')), may hold values from 0.1 to 1
- resting_trigger_level: float32 [16384], P(('blk', 'dp')), may hold values from 0.5 to 1.5
- pulse_sensitivity: float32 [4, 16384, 128], P(None, ('blk', 'dp')), may hold values from -6 to 6
- volt_cot: float32 [16384, 128], P(('blk', 'dp')), may hold values from -6 to 6
- adapt_cot: float32 [16384, 128], P(('blk', 'dp')), may hold values from -6 to 6
Outputs:
- volt_adj: float32 [16384, 128], P(('blk', 'dp'))
- adapt_adj: float32 [16384, 128], P(('blk', 'dp'))
- weight_grad: float32 [16384, 16384], P('blk', 'dp')
The draws below stay inside these ranges and needn't reach their ends.
Inputs may be any that keep to these rules, and one draw needn't show every extreme that they name: `spikes`: every entry is 0 or 1.
All inputs are finite; a program needn't handle non-finite values.
Results may differ from the reference program's by a relative error of at most 0.0024.
Values may be sent and summed in bfloat16 or wider, within the bound.
No kernel may reach another device: no remote copies, remote signals or barrier semaphores. Data moves between devices by JAX's collectives and lax.ppermute only.
A program may use at most 64 MiB of HBM per device.

```python
import math
import jax
import jax.numpy as jnp
from jax import lax

NEURON_TOTAL = 16384
TRIALS = 128
STEPS = 4
SLICE = 32
N_BLK = 16
N_DP = 32


def draw_spikes(key, part):
    omission_share_seed, fire_key = jax.random.split(jax.random.fold_in(key, 11))
    emitted_indicator = 0.03 * jnp.exp(jax.random.uniform(omission_share_seed, (NEURON_TOTAL,), jnp.float32) * math.log(0.5 / 0.03))
    pulse_likelihood = jax.random.uniform(fire_key, (STEPS, NEURON_TOTAL, TRIALS), jnp.float32)
    return jnp.where(pulse_likelihood < emitted_indicator[None, :, None], 1.0, 0.0).astype(jnp.bfloat16)


def shard_levels(stream_key, dims, pieces, least, top_value):
    loudness, own = 1.0, jax.random.fold_in(stream_key, 6)
    for dim, shards_of in pieces:
        heights = jnp.exp(jax.random.uniform(jax.random.fold_in(own, dim), (shards_of,), jnp.float32, least / len(pieces), top_value / len(pieces)))
        loudness = loudness * jnp.repeat(heights, dims[dim] // shards_of).reshape([-1 if axis == dim else 1 for axis in range(len(dims))])
    return loudness


def bell_draw(stream_key, extent, scale, limit, pieces=(), held_as=jnp.bfloat16):
    entries = jax.random.normal(stream_key, extent, jnp.float32) * scale
    if len(pieces) > 0:
        entries = shard_levels(stream_key, extent, pieces, -0.22, 0.18) * entries
    return jnp.clip(entries, min=-limit, max=limit).astype(held_as)


def setup_inputs(seed: int = 0) -> dict:
    streams_of = jax.random.split(jax.random.key(seed), 13)
    return {
        "spikes": draw_spikes(jax.random.fold_in(streams_of[12], 71), 0),
        "rec_weights": bell_draw(streams_of[1], (NEURON_TOTAL, NEURON_TOTAL), NEURON_TOTAL ** -0.5, 0.046875, ((0, 16), (1, 32))),
        "in_current": bell_draw(streams_of[2], (STEPS, NEURON_TOTAL, TRIALS), 1.0, 6.0, ((1, 512),), jnp.float32),
        "volt_init": bell_draw(streams_of[3], (NEURON_TOTAL, TRIALS), 1.0, 6.0, ((0, 512),), jnp.float32),
        "adapt_init": jnp.clip(3.0 * jax.random.uniform(streams_of[4], (NEURON_TOTAL, TRIALS), jnp.float32) ** shard_levels(streams_of[4], (NEURON_TOTAL, TRIALS), ((0, 512),), -0.2, 0.2), 0.0, 3.0),
        "mem_decay": jnp.clip(0.5 + 0.47000003 * jax.random.uniform(streams_of[5], (NEURON_TOTAL,), jnp.float32) ** shard_levels(streams_of[5], (NEURON_TOTAL,), ((0, 512),), -0.2, 0.2), 0.5, 0.97),
        "adapt_decay": jnp.clip(0.7 + 0.29000002 * jax.random.uniform(streams_of[6], (NEURON_TOTAL,), jnp.float32) ** shard_levels(streams_of[6], (NEURON_TOTAL,), ((0, 512),), -0.2, 0.2), 0.7, 0.99),
        "adapt_gain": jnp.clip(jnp.exp(math.log(1.0) - 2.3025851 * jax.random.uniform(streams_of[7], (NEURON_TOTAL,), jnp.float32) ** shard_levels(streams_of[7], (NEURON_TOTAL,), ((0, 512),), -0.2, 0.2)), 0.1, 1.0),
        "resting_trigger_level": jnp.clip(0.5 + 1.0 * jax.random.uniform(streams_of[8], (NEURON_TOTAL,), jnp.float32) ** shard_levels(streams_of[8], (NEURON_TOTAL,), ((0, 512),), -0.2, 0.2), 0.5, 1.5),
        "pulse_sensitivity": bell_draw(streams_of[9], (STEPS, NEURON_TOTAL, TRIALS), 1.0, 6.0, ((1, 512),), jnp.float32),
        "volt_cot": bell_draw(streams_of[10], (NEURON_TOTAL, TRIALS), 1.0, 6.0, ((0, 512),), jnp.float32),
        "adapt_cot": bell_draw(streams_of[11], (NEURON_TOTAL, TRIALS), 1.0, 6.0, ((0, 512),), jnp.float32),
    }


pseudo_derivative_factor = 0.5


def to_neurons(columns):
    return columns.reshape(N_DP, N_BLK, SLICE, -1).transpose(1, 0, 2, 3).reshape(NEURON_TOTAL, -1)


def to_columns(neurons):
    return neurons.reshape(N_BLK, N_DP, SLICE, -1).transpose(1, 0, 2, 3).reshape(NEURON_TOTAL, -1)


def reference(spikes, rec_weights, in_current, volt_init, adapt_init, mem_decay, adapt_decay, adapt_gain, resting_trigger_level, pulse_sensitivity, volt_cot, adapt_cot):
    leak_rate = mem_decay[:, None]
    keep_rate = adapt_decay[:, None]
    gain_col = adapt_gain[:, None]
    minimum_column = resting_trigger_level[:, None]
    voltage = volt_init
    adaptation = adapt_init
    threshold_values = []
    surrogates = []
    for moment in range(STEPS):
        current = to_neurons(lax.dot_general(rec_weights, spikes[moment], (((0,), (0,)), ((), ())), preferred_element_type=jnp.float32))
        thresh = minimum_column + gain_col * adaptation
        surrogate = pseudo_derivative_factor / jnp.square(1.0 + jnp.abs(voltage - thresh))
        fired = spikes[moment].astype(jnp.float32)
        voltage = leak_rate * voltage + current + in_current[moment] - thresh * fired
        adaptation = keep_rate * adaptation + fired
        threshold_values.append(thresh)
        surrogates.append(surrogate)
    volt_adj = volt_cot
    adapt_adj = adapt_cot
    weight_sum = jnp.zeros((NEURON_TOTAL, NEURON_TOTAL), jnp.float32)
    for moment in reversed(range(STEPS)):
        rounded = to_columns(volt_adj.astype(jnp.bfloat16))
        recurrent_matrix = jnp.dot(rec_weights, rounded, preferred_element_type=jnp.float32)
        weight_sum = weight_sum + lax.dot_general(spikes[moment], rounded, (((1,), (1,)), ((), ())), preferred_element_type=jnp.float32)
        fired = spikes[moment].astype(jnp.float32)
        spike_adj = pulse_sensitivity[moment] + recurrent_matrix - threshold_values[moment] * volt_adj + adapt_adj
        through = surrogates[moment] * spike_adj
        new_volt = leak_rate * volt_adj + through
        adapt_adj = keep_rate * adapt_adj - gain_col * (fired * volt_adj + through)
        volt_adj = new_volt
    return (volt_adj, adapt_adj, weight_sum)
```

```python
import jax
import jax.numpy as jnp
from jax import lax
from jax.sharding import PartitionSpec as P

pseudo_derivative_factor = 0.5
bf16 = jnp.bfloat16
f32 = jnp.float32


def exchange(parts, axis):
    return lax.all_to_all(parts, axis, 0, 0, tiled=True)


def row_partials(weights, pieces, num_dp):
    part = jnp.dot(weights, pieces, preferred_element_type=f32).astype(bf16)
    return part.reshape(num_dp, -1, part.shape[-1])


def body(
    spikes,
    rec_weights,
    in_current,
    volt_init,
    adapt_init,
    mem_decay,
    adapt_decay,
    adapt_gain,
    resting_trigger_level,
    pulse_sensitivity,
    volt_cot,
    adapt_cot,
):
    num_steps = spikes.shape[0]
    own, trials = volt_init.shape
    num_blk = lax.axis_size("blk")
    num_dp = lax.axis_size("dp")
    own_fired = lax.dynamic_slice_in_dim(
        spikes, lax.axis_index("dp") * own, own, 1
    ).astype(f32)
    leak_rate = mem_decay[:, None]
    keep_rate = adapt_decay[:, None]
    gain_col = adapt_gain[:, None]
    minimum_column = resting_trigger_level[:, None]

    outgoing = [
        lax.dot_general(
            rec_weights, spikes[t], (((0,), (0,)), ((), ())), preferred_element_type=f32
        )
        .astype(bf16)
        .reshape(num_blk, 1, own, trials)
        for t in range(num_steps - 1)
    ]
    outgoing.append(
        jnp.broadcast_to(volt_cot.astype(bf16), (num_blk, 1, own, trials))
    )
    arrived = exchange(jnp.concatenate(outgoing, axis=1), "blk")
    currents = jnp.sum(arrived[:, : num_steps - 1].astype(f32), axis=0)
    pieces = arrived[:, num_steps - 1].reshape(num_blk * own, trials)

    voltage = volt_init
    adaptation = adapt_init
    threshold_values = []
    surrogates = []
    for t in range(num_steps):
        thresh = minimum_column + gain_col * adaptation
        surrogates.append(
            pseudo_derivative_factor / jnp.square(1.0 + jnp.abs(voltage - thresh))
        )
        threshold_values.append(thresh)
        if t + 1 < num_steps:
            voltage = (
                leak_rate * voltage + currents[t] + in_current[t] - thresh * own_fired[t]
            )
            adaptation = keep_rate * adaptation + own_fired[t]

    volt_adj = volt_cot
    adapt_adj = adapt_cot
    kept_pieces = []
    for t in reversed(range(num_steps)):
        kept_pieces.insert(0, pieces)
        partials = exchange(row_partials(rec_weights, pieces, num_dp), "dp")
        recurrent = jnp.sum(partials.astype(f32), axis=0)
        spike_adj = (
            pulse_sensitivity[t]
            + recurrent
            - threshold_values[t] * volt_adj
            + adapt_adj
        )
        through = surrogates[t] * spike_adj
        new_volt = leak_rate * volt_adj + through
        adapt_adj = keep_rate * adapt_adj - gain_col * (own_fired[t] * volt_adj + through)
        volt_adj = new_volt
        if t > 0:
            copies = jnp.broadcast_to(volt_adj.astype(bf16), (num_blk, own, trials))
            pieces = exchange(copies, "blk").reshape(num_blk * own, trials)
    weight_sum = jnp.einsum(
        "tpb,tcb->pc", spikes, jnp.stack(kept_pieces), preferred_element_type=f32
    )
    return (volt_adj, adapt_adj, weight_sum)


def solution(mesh):
    own = P(("blk", "dp"))
    window = P(None, ("blk", "dp"))
    return jax.shard_map(
        body,
        mesh=mesh,
        in_specs=(
            P(None, "blk"),
            P("blk", "dp"),
            window,
            own,
            own,
            own,
            own,
            own,
            own,
            window,
            own,
            own,
        ),
        out_specs=(own, own, P("blk", "dp")),
        check_vma=False,
    )
```

```python
import jax
import jax.numpy as jnp
from jax import lax
from jax.sharding import PartitionSpec as P

pseudo_derivative_factor = 0.5
bf16 = jnp.bfloat16
f32 = jnp.float32


def exchange(parts, axis):
    return lax.all_to_all(parts, axis, 0, 0, tiled=True)


def row_partials(weights, pieces, num_dp):
    part = jnp.dot(weights, pieces, preferred_element_type=f32).astype(bf16)
    return part.reshape(num_dp, -1, part.shape[-1])


def halve(total, bit):
    size = lax.axis_size("blk")
    mine = (lax.axis_index("blk") // bit) % 2
    pairs = total.reshape(total.shape[0] // 2, 2, *total.shape[1:])
    sent = jnp.where(mine == 0, pairs[:, 1], pairs[:, 0]).astype(bf16)
    got = lax.ppermute(sent, "blk", [(s, s ^ bit) for s in range(size)])
    kept = jnp.where(mine == 0, pairs[:, 0], pairs[:, 1])
    return kept + got.astype(f32)


def body(
    spikes,
    rec_weights,
    in_current,
    volt_init,
    adapt_init,
    mem_decay,
    adapt_decay,
    adapt_gain,
    resting_trigger_level,
    pulse_sensitivity,
    volt_cot,
    adapt_cot,
):
    num_steps = spikes.shape[0]
    own, trials = volt_init.shape
    num_blk = lax.axis_size("blk")
    num_dp = lax.axis_size("dp")
    own_fired = lax.dynamic_slice_in_dim(
        spikes, lax.axis_index("dp") * own, own, 1
    ).astype(f32)
    leak_rate = mem_decay[:, None]
    keep_rate = adapt_decay[:, None]
    gain_col = adapt_gain[:, None]
    minimum_column = resting_trigger_level[:, None]

    def gathered(values):
        copies = jnp.broadcast_to(values.astype(bf16), (num_blk, own, trials))
        return exchange(copies, "blk").reshape(num_blk * own, trials)

    pieces = gathered(volt_cot)
    total = jnp.einsum(
        "pc,tpb->ctb",
        rec_weights,
        spikes[: num_steps - 1],
        preferred_element_type=f32,
    ).reshape(num_blk, own, num_steps - 1, trials)
    bit = 1
    while bit < num_blk:
        total = halve(total, bit)
        bit *= 2
    currents = total[0]
    partials = exchange(row_partials(rec_weights, pieces, num_dp), "dp")

    voltage = volt_init
    adaptation = adapt_init
    threshold_values = []
    surrogates = []
    for t in range(num_steps):
        thresh = minimum_column + gain_col * adaptation
        surrogates.append(
            pseudo_derivative_factor / jnp.square(1.0 + jnp.abs(voltage - thresh))
        )
        threshold_values.append(thresh)
        if t + 1 < num_steps:
            voltage = (
                leak_rate * voltage
                + currents[:, t]
                + in_current[t]
                - thresh * own_fired[t]
            )
            adaptation = keep_rate * adaptation + own_fired[t]

    volt_adj = volt_cot
    adapt_adj = adapt_cot
    kept_pieces = []
    for t in reversed(range(num_steps)):
        kept_pieces.insert(0, pieces)
        if t + 1 < num_steps:
            partials = exchange(row_partials(rec_weights, pieces, num_dp), "dp")
        known = pulse_sensitivity[t] - threshold_values[t] * volt_adj + adapt_adj
        volt_known = leak_rate * volt_adj + surrogates[t] * known
        adapt_known = keep_rate * adapt_adj - gain_col * (
            own_fired[t] * volt_adj + surrogates[t] * known
        )
        recurrent = jnp.sum(partials.astype(f32), axis=0)
        volt_adj = volt_known + surrogates[t] * recurrent
        adapt_adj = adapt_known - gain_col * surrogates[t] * recurrent
        if t > 0:
            pieces = gathered(volt_adj)
    weight_sum = jnp.einsum(
        "tpb,tcb->pc", spikes, jnp.stack(kept_pieces), preferred_element_type=f32
    )
    return (volt_adj, adapt_adj, weight_sum)


def solution(mesh):
    own = P(("blk", "dp"))
    window = P(None, ("blk", "dp"))
    return jax.shard_map(
        body,
        mesh=mesh,
        in_specs=(
            P(None, "blk"),
            P("blk", "dp"),
            window,
            own,
            own,
            own,
            own,
            own,
            own,
            window,
            own,
            own,
        ),
        out_specs=(own, own, P("blk", "dp")),
        check_vma=False,
    )
```

```python
import jax
import jax.numpy as jnp
from jax import lax
from jax.sharding import PartitionSpec as P

pseudo_derivative_factor = 0.5
bf16 = jnp.bfloat16
f32 = jnp.float32


def exchange(parts, axis):
    return lax.all_to_all(parts, axis, 0, 0, tiled=True)


def row_partials(weights, pieces, num_dp):
    part = jnp.dot(weights, pieces, preferred_element_type=f32).astype(bf16)
    return part.reshape(num_dp, -1, part.shape[-1])


def body(
    spikes,
    rec_weights,
    in_current,
    volt_init,
    adapt_init,
    mem_decay,
    adapt_decay,
    adapt_gain,
    resting_trigger_level,
    pulse_sensitivity,
    volt_cot,
    adapt_cot,
):
    num_steps = spikes.shape[0]
    own, trials = volt_init.shape
    num_blk = lax.axis_size("blk")
    num_dp = lax.axis_size("dp")
    own_fired = lax.dynamic_slice_in_dim(
        spikes, lax.axis_index("dp") * own, own, 1
    ).astype(f32)
    leak_rate = mem_decay[:, None]
    keep_rate = adapt_decay[:, None]
    gain_col = adapt_gain[:, None]
    minimum_column = resting_trigger_level[:, None]

    sums = jnp.einsum(
        "pc,tpb->ctb", rec_weights, spikes[: num_steps - 1], preferred_element_type=f32
    ).astype(bf16)
    sums = sums.reshape(num_blk, own, num_steps - 1, trials).swapaxes(1, 2)
    copies = jnp.broadcast_to(volt_cot.astype(bf16), (num_blk, 1, own, trials))
    arrived = exchange(jnp.concatenate([sums, copies], axis=1), "blk")
    currents = jnp.sum(arrived[:, : num_steps - 1].astype(f32), axis=0)
    pieces = arrived[:, num_steps - 1].reshape(num_blk * own, trials)

    voltage = volt_init
    adaptation = adapt_init
    threshold_values = []
    surrogates = []
    for t in range(num_steps):
        thresh = minimum_column + gain_col * adaptation
        surrogates.append(
            pseudo_derivative_factor / jnp.square(1.0 + jnp.abs(voltage - thresh))
        )
        threshold_values.append(thresh)
        if t + 1 < num_steps:
            voltage = (
                leak_rate * voltage + currents[t] + in_current[t] - thresh * own_fired[t]
            )
            adaptation = keep_rate * adaptation + own_fired[t]

    volt_adj = volt_cot
    adapt_adj = adapt_cot
    kept_pieces = []
    for t in reversed(range(num_steps)):
        kept_pieces.insert(0, pieces)
        partials = exchange(row_partials(rec_weights, pieces, num_dp), "dp")
        known = pulse_sensitivity[t] - threshold_values[t] * volt_adj + adapt_adj
        volt_known = leak_rate * volt_adj + surrogates[t] * known
        adapt_known = keep_rate * adapt_adj - gain_col * (
            own_fired[t] * volt_adj + surrogates[t] * known
        )
        slope = gain_col * surrogates[t]
        if t == 0:
            volt_known, adapt_known, slope = lax.optimization_barrier(
                (volt_known, adapt_known, slope)
            )
        recurrent = jnp.sum(partials.astype(f32), axis=0)
        volt_adj = volt_known + surrogates[t] * recurrent
        adapt_adj = adapt_known - slope * recurrent
        if t > 0:
            copies = jnp.broadcast_to(volt_adj.astype(bf16), (num_blk, own, trials))
            pieces = exchange(copies, "blk").reshape(num_blk * own, trials)
    weight_sum = jnp.einsum(
        "tpb,tcb->pc", spikes, jnp.stack(kept_pieces), preferred_element_type=f32
    )
    return (volt_adj, adapt_adj, weight_sum)


def solution(mesh):
    own = P(("blk", "dp"))
    window = P(None, ("blk", "dp"))
    return jax.shard_map(
        body,
        mesh=mesh,
        in_specs=(
            P(None, "blk"),
            P("blk", "dp"),
            window,
            own,
            own,
            own,
            own,
            own,
            own,
            window,
            own,
            own,
        ),
        out_specs=(own, own, P("blk", "dp")),
        check_vma=False,
    )
```

```python
import jax
import jax.numpy as jnp
from jax import lax
from jax.sharding import PartitionSpec as P

pseudo_derivative_factor = 0.5
bf16 = jnp.bfloat16
f32 = jnp.float32


def exchange(parts, axis):
    return lax.all_to_all(parts, axis, 0, 0, tiled=True)


def row_partials(weights, pieces, num_dp):
    part = jnp.dot(weights, pieces, preferred_element_type=f32).astype(bf16)
    return part.reshape(num_dp, -1, part.shape[-1])


def body(
    spikes,
    rec_weights,
    in_current,
    volt_init,
    adapt_init,
    mem_decay,
    adapt_decay,
    adapt_gain,
    resting_trigger_level,
    pulse_sensitivity,
    volt_cot,
    adapt_cot,
):
    num_steps = spikes.shape[0]
    own, trials = volt_init.shape
    num_blk = lax.axis_size("blk")
    num_dp = lax.axis_size("dp")
    own_fired = lax.dynamic_slice_in_dim(
        spikes, lax.axis_index("dp") * own, own, 1
    ).astype(f32)
    leak_rate = mem_decay[:, None]
    keep_rate = adapt_decay[:, None]
    gain_col = adapt_gain[:, None]
    minimum_column = resting_trigger_level[:, None]

    early = lax.optimization_barrier(spikes[: num_steps - 1])
    sums = jnp.einsum(
        "pc,tpb->ctb", rec_weights, early, preferred_element_type=f32
    ).astype(bf16)
    sums = sums.reshape(num_blk, own, num_steps - 1, trials).swapaxes(1, 2)
    copies = jnp.broadcast_to(volt_cot.astype(bf16), (num_blk, 1, own, trials))
    arrived = exchange(jnp.concatenate([sums, copies], axis=1), "blk")
    currents = jnp.sum(arrived[:, : num_steps - 1].astype(f32), axis=0)
    pieces = arrived[:, num_steps - 1].reshape(num_blk * own, trials)

    def threshold(adaptation):
        return minimum_column + gain_col * adaptation

    def surrogate_of(voltage, thresh):
        return pseudo_derivative_factor / jnp.square(1.0 + jnp.abs(voltage - thresh))

    voltage = volt_init
    adaptation = adapt_init
    threshold_values = []
    surrogates = []
    for t in range(num_steps):
        thresh = threshold(adaptation)
        surrogates.append(surrogate_of(voltage, thresh))
        threshold_values.append(thresh)
        if t + 1 < num_steps:
            voltage = (
                leak_rate * voltage + currents[t] + in_current[t] - thresh * own_fired[t]
            )
            adaptation = keep_rate * adaptation + own_fired[t]

    volt_adj = volt_cot
    adapt_adj = adapt_cot
    kept_pieces = []
    for t in reversed(range(num_steps)):
        if t == 0:
            pieces, first_volt, first_adapt = lax.optimization_barrier(
                (pieces, volt_init, adapt_init)
            )
            thresh = threshold(first_adapt)
            surrogate = surrogate_of(first_volt, thresh)
        kept_pieces.insert(0, pieces)
        partials = exchange(row_partials(rec_weights, pieces, num_dp), "dp")
        if t > 0:
            thresh, surrogate = threshold_values[t], surrogates[t]
        known = pulse_sensitivity[t] - thresh * volt_adj + adapt_adj
        volt_known = leak_rate * volt_adj + surrogate * known
        adapt_known = keep_rate * adapt_adj - gain_col * (
            own_fired[t] * volt_adj + surrogate * known
        )
        slope = gain_col * surrogate
        if t == 0:
            volt_known, adapt_known, surrogate, slope = lax.optimization_barrier(
                (volt_known, adapt_known, surrogate, slope)
            )
        recurrent = jnp.sum(partials.astype(f32), axis=0)
        volt_adj = volt_known + surrogate * recurrent
        adapt_adj = adapt_known - slope * recurrent
        if t > 0:
            copies = jnp.broadcast_to(volt_adj.astype(bf16), (num_blk, own, trials))
            pieces = exchange(copies, "blk").reshape(num_blk * own, trials)
    weight_sum = jnp.einsum(
        "tpb,tcb->pc", spikes, jnp.stack(kept_pieces), preferred_element_type=f32
    )
    return (volt_adj, adapt_adj, weight_sum)


def solution(mesh):
    own = P(("blk", "dp"))
    window = P(None, ("blk", "dp"))
    return jax.shard_map(
        body,
        mesh=mesh,
        in_specs=(
            P(None, "blk"),
            P("blk", "dp"),
            window,
            own,
            own,
            own,
            own,
            own,
            own,
            window,
            own,
            own,
        ),
        out_specs=(own, own, P("blk", "dp")),
        check_vma=False,
    )
```

```python
import jax
import jax.numpy as jnp
from jax import lax
from jax.sharding import PartitionSpec as P

pseudo_derivative_factor = 0.5
bf16 = jnp.bfloat16
f32 = jnp.float32


def exchange(parts, axis):
    return lax.all_to_all(parts, axis, 0, 0, tiled=True)


def row_partials(weights, pieces, num_dp):
    rows, cols = weights.shape
    return jnp.einsum(
        "kpc,cb->kpb",
        weights.reshape(num_dp, rows // num_dp, cols),
        pieces,
        preferred_element_type=f32,
    ).astype(bf16)


def body(
    spikes,
    rec_weights,
    in_current,
    volt_init,
    adapt_init,
    mem_decay,
    adapt_decay,
    adapt_gain,
    resting_trigger_level,
    pulse_sensitivity,
    volt_cot,
    adapt_cot,
):
    num_steps = spikes.shape[0]
    own, trials = volt_init.shape
    num_blk = lax.axis_size("blk")
    num_dp = lax.axis_size("dp")
    own_fired = lax.dynamic_slice_in_dim(
        spikes, lax.axis_index("dp") * own, own, 1
    ).astype(f32)
    leak_rate = mem_decay[:, None]
    keep_rate = adapt_decay[:, None]
    gain_col = adapt_gain[:, None]
    minimum_column = resting_trigger_level[:, None]

    early = lax.optimization_barrier(spikes[: num_steps - 1])
    sums = jnp.einsum(
        "pc,tpb->ctb", rec_weights, early, preferred_element_type=f32
    ).astype(bf16)
    sums, last_adj = lax.optimization_barrier((sums, volt_cot))
    sums = sums.reshape(num_blk, own, num_steps - 1, trials).swapaxes(1, 2)
    copies = jnp.broadcast_to(last_adj.astype(bf16), (num_blk, 1, own, trials))
    arrived = exchange(jnp.concatenate([sums, copies], axis=1), "blk")
    currents = jnp.sum(arrived[:, : num_steps - 1].astype(f32), axis=0)
    pieces = arrived[:, num_steps - 1].reshape(num_blk * own, trials)

    def threshold(adaptation):
        return minimum_column + gain_col * adaptation

    def surrogate_of(voltage, thresh):
        return pseudo_derivative_factor / jnp.square(1.0 + jnp.abs(voltage - thresh))

    voltage = volt_init
    adaptation = adapt_init
    threshold_values = []
    surrogates = []
    for t in range(num_steps):
        thresh = threshold(adaptation)
        surrogates.append(surrogate_of(voltage, thresh))
        threshold_values.append(thresh)
        if t + 1 < num_steps:
            voltage = (
                leak_rate * voltage + currents[t] + in_current[t] - thresh * own_fired[t]
            )
            adaptation = keep_rate * adaptation + own_fired[t]

    volt_adj = volt_cot
    adapt_adj = adapt_cot
    kept_pieces = []
    for t in reversed(range(num_steps)):
        if t == 0:
            pieces, first_volt, first_adapt = lax.optimization_barrier(
                (pieces, volt_init, adapt_init)
            )
            thresh = threshold(first_adapt)
            surrogate = surrogate_of(first_volt, thresh)
        kept_pieces.insert(0, pieces)
        partials = exchange(row_partials(rec_weights, pieces, num_dp), "dp")
        if t > 0:
            thresh, surrogate = threshold_values[t], surrogates[t]
        known = pulse_sensitivity[t] - thresh * volt_adj + adapt_adj
        volt_known = leak_rate * volt_adj + surrogate * known
        adapt_known = keep_rate * adapt_adj - gain_col * (
            own_fired[t] * volt_adj + surrogate * known
        )
        slope = gain_col * surrogate
        if t == 0:
            volt_known, adapt_known, surrogate, slope = lax.optimization_barrier(
                (volt_known, adapt_known, surrogate, slope)
            )
        recurrent = jnp.sum(partials.astype(f32), axis=0)
        volt_adj = volt_known + surrogate * recurrent
        adapt_adj = adapt_known - slope * recurrent
        if t > 0:
            copies = jnp.broadcast_to(volt_adj.astype(bf16), (num_blk, own, trials))
            pieces = exchange(copies, "blk").reshape(num_blk * own, trials)
    weight_sum = jnp.einsum(
        "tpb,tcb->pc", spikes, jnp.stack(kept_pieces), preferred_element_type=f32
    )
    return (volt_adj, adapt_adj, weight_sum)


def solution(mesh):
    own = P(("blk", "dp"))
    window = P(None, ("blk", "dp"))
    return jax.shard_map(
        body,
        mesh=mesh,
        in_specs=(
            P(None, "blk"),
            P("blk", "dp"),
            window,
            own,
            own,
            own,
            own,
            own,
            own,
            window,
            own,
            own,
        ),
        out_specs=(own, own, P("blk", "dp")),
        check_vma=False,
    )
```

```python
import jax
import jax.numpy as jnp
from jax import lax
from jax.sharding import PartitionSpec as P

pseudo_derivative_factor = 0.5
bf16 = jnp.bfloat16
f32 = jnp.float32


def leader(axis):
    size = lax.axis_size(axis)
    return size * 5 // 8 if axis == "dp" else size * 11 // 16


def rotated(parts, start):
    return jnp.concatenate([parts[start:], parts[:start]], axis=0)


def exchange(parts, axis):
    size = lax.axis_size(axis)
    order = [(leader(axis) + p) % size for p in range(size)]
    return lax.all_to_all(parts, axis, 0, 0, axis_index_groups=[order], tiled=True)


def by_member(parts, axis):
    return rotated(parts, lax.axis_size(axis) - leader(axis))


def row_partials(weights, pieces, num_dp):
    rows, cols = weights.shape
    part = jnp.einsum(
        "kpc,cb->kpb",
        weights.reshape(num_dp, rows // num_dp, cols),
        pieces,
        preferred_element_type=f32,
    ).astype(bf16)
    return rotated(part, leader("dp"))


def body(
    spikes,
    rec_weights,
    in_current,
    volt_init,
    adapt_init,
    mem_decay,
    adapt_decay,
    adapt_gain,
    resting_trigger_level,
    pulse_sensitivity,
    volt_cot,
    adapt_cot,
):
    num_steps = spikes.shape[0]
    own, trials = volt_init.shape
    num_blk = lax.axis_size("blk")
    num_dp = lax.axis_size("dp")
    own_fired = lax.dynamic_slice_in_dim(
        spikes, lax.axis_index("dp") * own, own, 1
    ).astype(f32)
    leak_rate = mem_decay[:, None]
    keep_rate = adapt_decay[:, None]
    gain_col = adapt_gain[:, None]
    minimum_column = resting_trigger_level[:, None]

    early = lax.optimization_barrier(spikes[: num_steps - 1])
    sums = jnp.einsum(
        "pc,tpb->ctb", rec_weights, early, preferred_element_type=f32
    ).astype(bf16)
    sums, last_adj = lax.optimization_barrier((sums, volt_cot))
    sums = sums.reshape(num_blk, own, num_steps - 1, trials).swapaxes(1, 2)
    sums = rotated(sums, leader("blk"))
    copies = jnp.broadcast_to(last_adj.astype(bf16), (num_blk, 1, own, trials))
    arrived = exchange(jnp.concatenate([sums, copies], axis=1), "blk")
    currents = jnp.sum(arrived[:, : num_steps - 1].astype(f32), axis=0)
    pieces = by_member(arrived[:, num_steps - 1], "blk").reshape(num_blk * own, trials)

    def threshold(adaptation):
        return minimum_column + gain_col * adaptation

    def surrogate_of(voltage, thresh):
        return pseudo_derivative_factor / jnp.square(1.0 + jnp.abs(voltage - thresh))

    voltage = volt_init
    adaptation = adapt_init
    threshold_values = []
    surrogates = []
    for t in range(num_steps):
        thresh = threshold(adaptation)
        surrogates.append(surrogate_of(voltage, thresh))
        threshold_values.append(thresh)
        if t + 1 < num_steps:
            voltage = (
                leak_rate * voltage + currents[t] + in_current[t] - thresh * own_fired[t]
            )
            adaptation = keep_rate * adaptation + own_fired[t]

    volt_adj = volt_cot
    adapt_adj = adapt_cot
    kept_pieces = []
    for t in reversed(range(num_steps)):
        if t == 0:
            pieces, first_volt, first_adapt = lax.optimization_barrier(
                (pieces, volt_init, adapt_init)
            )
            thresh = threshold(first_adapt)
            surrogate = surrogate_of(first_volt, thresh)
        kept_pieces.insert(0, pieces)
        partials = exchange(row_partials(rec_weights, pieces, num_dp), "dp")
        if t > 0:
            thresh, surrogate = threshold_values[t], surrogates[t]
        known = pulse_sensitivity[t] - thresh * volt_adj + adapt_adj
        volt_known = leak_rate * volt_adj + surrogate * known
        adapt_known = keep_rate * adapt_adj - gain_col * (
            own_fired[t] * volt_adj + surrogate * known
        )
        slope = gain_col * surrogate
        if t == 0:
            volt_known, adapt_known, surrogate, slope = lax.optimization_barrier(
                (volt_known, adapt_known, surrogate, slope)
            )
        recurrent = jnp.sum(partials.astype(f32), axis=0)
        volt_adj = volt_known + surrogate * recurrent
        adapt_adj = adapt_known - slope * recurrent
        if t > 0:
            copies = jnp.broadcast_to(volt_adj.astype(bf16), (num_blk, own, trials))
            pieces = by_member(exchange(copies, "blk"), "blk")
            pieces = pieces.reshape(num_blk * own, trials)
    weight_sum = jnp.einsum(
        "tpb,tcb->pc", spikes, jnp.stack(kept_pieces), preferred_element_type=f32
    )
    return (volt_adj, adapt_adj, weight_sum)


def solution(mesh):
    own = P(("blk", "dp"))
    window = P(None, ("blk", "dp"))
    return jax.shard_map(
        body,
        mesh=mesh,
        in_specs=(
            P(None, "blk"),
            P("blk", "dp"),
            window,
            own,
            own,
            own,
            own,
            own,
            own,
            window,
            own,
            own,
        ),
        out_specs=(own, own, P("blk", "dp")),
        check_vma=False,
    )
```

```python
import jax
import jax.numpy as jnp
from jax import lax
from jax.sharding import PartitionSpec as P

pseudo_derivative_factor = 0.5
bf16 = jnp.bfloat16
f32 = jnp.float32


def leader(axis):
    size = lax.axis_size(axis)
    return size * 5 // 8 if axis == "dp" else size * 11 // 16


def rotated(parts, start):
    return jnp.concatenate([parts[start:], parts[:start]], axis=0)


def exchange(parts, axis):
    size = lax.axis_size(axis)
    order = [(leader(axis) + p) % size for p in range(size)]
    return lax.all_to_all(parts, axis, 0, 0, axis_index_groups=[order], tiled=True)


def by_member(parts, axis):
    return rotated(parts, lax.axis_size(axis) - leader(axis))


def row_partials(weights, pieces, num_dp):
    rows, cols = weights.shape
    part = jnp.einsum(
        "kpc,cb->kpb",
        weights.reshape(num_dp, rows // num_dp, cols),
        pieces,
        preferred_element_type=f32,
    ).astype(bf16)
    return rotated(part, leader("dp"))


def body(
    spikes,
    rec_weights,
    in_current,
    volt_init,
    adapt_init,
    mem_decay,
    adapt_decay,
    adapt_gain,
    resting_trigger_level,
    pulse_sensitivity,
    volt_cot,
    adapt_cot,
):
    num_steps = spikes.shape[0]
    own, trials = volt_init.shape
    num_blk = lax.axis_size("blk")
    num_dp = lax.axis_size("dp")
    own_fired = lax.dynamic_slice_in_dim(
        spikes, lax.axis_index("dp") * own, own, 1
    ).astype(f32)
    leak_rate = mem_decay[:, None]
    keep_rate = adapt_decay[:, None]
    gain_col = adapt_gain[:, None]
    minimum_column = resting_trigger_level[:, None]

    early = lax.optimization_barrier(spikes[: num_steps - 1])
    sums = jnp.einsum(
        "pc,tpb->ctb", rec_weights, early, preferred_element_type=f32
    ).astype(bf16)
    sums, last_adj = lax.optimization_barrier((sums, volt_cot))
    sums = sums.reshape(num_blk, own, num_steps - 1, trials).swapaxes(1, 2)
    sums = rotated(sums, leader("blk"))
    copies = jnp.broadcast_to(last_adj.astype(bf16), (num_blk, 1, own, trials))
    arrived = exchange(jnp.concatenate([sums, copies], axis=1), "blk")
    currents = jnp.sum(arrived[:, : num_steps - 1].astype(f32), axis=0)
    pieces = by_member(arrived[:, num_steps - 1], "blk").reshape(num_blk * own, trials)

    def threshold(adaptation):
        return minimum_column + gain_col * adaptation

    def surrogate_of(voltage, thresh):
        return pseudo_derivative_factor / jnp.square(1.0 + jnp.abs(voltage - thresh))

    voltage = volt_init
    adaptation = adapt_init
    threshold_values = []
    surrogates = []
    for t in range(num_steps):
        thresh = threshold(adaptation)
        surrogates.append(surrogate_of(voltage, thresh))
        threshold_values.append(thresh)
        if t + 1 < num_steps:
            voltage = (
                leak_rate * voltage + currents[t] + in_current[t] - thresh * own_fired[t]
            )
            adaptation = keep_rate * adaptation + own_fired[t]

    volt_adj = volt_cot
    adapt_adj = adapt_cot
    kept_pieces = []
    for t in reversed(range(num_steps)):
        if t == 0:
            pieces, first_volt, first_adapt = lax.optimization_barrier(
                (pieces, volt_init, adapt_init)
            )
            thresh = threshold(first_adapt)
            surrogate = surrogate_of(first_volt, thresh)
        kept_pieces.insert(0, pieces)
        partials = exchange(row_partials(rec_weights, pieces, num_dp), "dp")
        if t > 0:
            thresh, surrogate = threshold_values[t], surrogates[t]
        known = pulse_sensitivity[t] - thresh * volt_adj + adapt_adj
        volt_known = leak_rate * volt_adj + surrogate * known
        adapt_known = keep_rate * adapt_adj - gain_col * (
            own_fired[t] * volt_adj + surrogate * known
        )
        slope = gain_col * surrogate
        if t == 0:
            volt_known, adapt_known, surrogate, slope = lax.optimization_barrier(
                (volt_known, adapt_known, surrogate, slope)
            )
        recurrent = jnp.sum(partials.astype(f32), axis=0)
        volt_adj = volt_known + surrogate * recurrent
        adapt_adj = adapt_known - slope * recurrent
        if t > 0:
            copies = jnp.broadcast_to(volt_adj.astype(bf16), (num_blk, own, trials))
            pieces = by_member(exchange(copies, "blk"), "blk")
            pieces = pieces.reshape(num_blk * own, trials)
    weight_sum = jnp.einsum(
        "tkpb,tcb->kpc",
        spikes.reshape(num_steps, num_dp, -1, trials),
        jnp.stack(kept_pieces),
        preferred_element_type=f32,
    ).reshape(rec_weights.shape)
    return (volt_adj, adapt_adj, weight_sum)


def solution(mesh):
    own = P(("blk", "dp"))
    window = P(None, ("blk", "dp"))
    return jax.shard_map(
        body,
        mesh=mesh,
        in_specs=(
            P(None, "blk"),
            P("blk", "dp"),
            window,
            own,
            own,
            own,
            own,
            own,
            own,
            window,
            own,
            own,
        ),
        out_specs=(own, own, P("blk", "dp")),
        check_vma=False,
    )
```

```python
import jax
import jax.numpy as jnp
from jax import lax
from jax.sharding import PartitionSpec as P

pseudo_derivative_factor = 0.5
bf16 = jnp.bfloat16
f32 = jnp.float32


def leader(axis):
    return lax.axis_size(axis) * 5 // 8


def rotated(parts, start):
    return jnp.concatenate([parts[start:], parts[:start]], axis=0)


def exchange(parts, axis):
    size = lax.axis_size(axis)
    order = [(leader(axis) + p) % size for p in range(size)]
    return lax.all_to_all(parts, axis, 0, 0, axis_index_groups=[order], tiled=True)


def by_member(parts, axis):
    return rotated(parts, lax.axis_size(axis) - leader(axis))


def row_partials(weights, pieces, num_dp):
    rows, cols = weights.shape
    part = jnp.einsum(
        "kpc,cb->kpb",
        weights.reshape(num_dp, rows // num_dp, cols),
        pieces,
        preferred_element_type=f32,
    ).astype(bf16)
    return rotated(part, leader("dp"))


def body(
    spikes,
    rec_weights,
    in_current,
    volt_init,
    adapt_init,
    mem_decay,
    adapt_decay,
    adapt_gain,
    resting_trigger_level,
    pulse_sensitivity,
    volt_cot,
    adapt_cot,
):
    num_steps = spikes.shape[0]
    own, trials = volt_init.shape
    num_blk = lax.axis_size("blk")
    num_dp = lax.axis_size("dp")
    leak_rate = mem_decay[:, None]
    keep_rate = adapt_decay[:, None]
    gain_col = adapt_gain[:, None]
    minimum_column = resting_trigger_level[:, None]

    early = lax.optimization_barrier(spikes[: num_steps - 1])
    sums = jnp.einsum(
        "pc,tpb->ctb", rec_weights, early, preferred_element_type=f32
    ).astype(bf16)
    sums, last_adj, own_start = lax.optimization_barrier(
        (sums, volt_cot, lax.axis_index("dp") * own)
    )
    sums = sums.reshape(num_blk, own, num_steps - 1, trials).swapaxes(1, 2)
    sums = rotated(sums, leader("blk"))
    copies = jnp.broadcast_to(last_adj.astype(bf16), (num_blk, 1, own, trials))
    arrived = exchange(jnp.concatenate([sums, copies], axis=1), "blk")
    arrived, late_spikes = lax.optimization_barrier((arrived, spikes))
    own_fired = lax.dynamic_slice_in_dim(
        late_spikes, own_start, own, 1, allow_negative_indices=False
    ).astype(f32)
    currents = jnp.sum(arrived[:, : num_steps - 1].astype(f32), axis=0)
    pieces = by_member(arrived[:, num_steps - 1], "blk").reshape(num_blk * own, trials)

    def threshold(adaptation):
        return minimum_column + gain_col * adaptation

    def surrogate_of(voltage, thresh):
        return pseudo_derivative_factor / jnp.square(1.0 + jnp.abs(voltage - thresh))

    voltage = volt_init
    adaptation = adapt_init
    threshold_values = []
    surrogates = []
    for t in range(num_steps):
        thresh = threshold(adaptation)
        surrogates.append(surrogate_of(voltage, thresh))
        threshold_values.append(thresh)
        if t + 1 < num_steps:
            voltage = (
                leak_rate * voltage + currents[t] + in_current[t] - thresh * own_fired[t]
            )
            adaptation = keep_rate * adaptation + own_fired[t]

    volt_adj = volt_cot
    adapt_adj = adapt_cot
    kept_pieces = []
    outgoing = row_partials(rec_weights, pieces, num_dp)
    outgoing, surrogates, threshold_values, own_fired = lax.optimization_barrier(
        (outgoing, surrogates, threshold_values, own_fired)
    )
    for t in reversed(range(num_steps)):
        if t == 0:
            pieces, first_volt, first_adapt = lax.optimization_barrier(
                (pieces, volt_init, adapt_init)
            )
            thresh = threshold(first_adapt)
            surrogate = surrogate_of(first_volt, thresh)
        kept_pieces.insert(0, pieces)
        if t + 1 < num_steps:
            outgoing = row_partials(rec_weights, pieces, num_dp)
        partials = exchange(outgoing, "dp")
        if t > 0:
            thresh, surrogate = threshold_values[t], surrogates[t]
        known = pulse_sensitivity[t] - thresh * volt_adj + adapt_adj
        volt_known = leak_rate * volt_adj + surrogate * known
        adapt_known = keep_rate * adapt_adj - gain_col * (
            own_fired[t] * volt_adj + surrogate * known
        )
        slope = gain_col * surrogate
        if t == 0:
            volt_known, adapt_known, surrogate, slope = lax.optimization_barrier(
                (volt_known, adapt_known, surrogate, slope)
            )
        recurrent = jnp.sum(partials.astype(f32), axis=0)
        volt_adj = volt_known + surrogate * recurrent
        adapt_adj = adapt_known - slope * recurrent
        if t > 0:
            copies = jnp.broadcast_to(volt_adj.astype(bf16), (num_blk, own, trials))
            pieces = by_member(exchange(copies, "blk"), "blk")
            pieces = pieces.reshape(num_blk * own, trials)
    weight_sum = jnp.einsum(
        "tkpb,tcb->kpc",
        late_spikes.reshape(num_steps, num_dp, -1, trials),
        jnp.stack(kept_pieces),
        preferred_element_type=f32,
    ).reshape(rec_weights.shape)
    return (volt_adj, adapt_adj, weight_sum)


def solution(mesh):
    own = P(("blk", "dp"))
    window = P(None, ("blk", "dp"))
    return jax.shard_map(
        body,
        mesh=mesh,
        in_specs=(
            P(None, "blk"),
            P("blk", "dp"),
            window,
            own,
            own,
            own,
            own,
            own,
            own,
            window,
            own,
            own,
        ),
        out_specs=(own, own, P("blk", "dp")),
        check_vma=False,
    )
```
